32 devices in a mesh: tm: 2 (over core), tile: 16 (over z, y, x).
Axes of the slice: x: 2, y: 2, z: 4, core: 2. Of those that a mesh axis runs over, the one named last changes fastest.
Arguments:
- features: bfloat16 [1, 8, 64, 64, 192], P(None, 'tm', 'tile'), may hold values from -60 to 60
- gain_one: float32 [192], replicated, may hold values from 0.5 to 1.5
- shift_one: float32 [192], replicated, may hold values from -3 to 3
- kernel_one: bfloat16 [3, 3, 3, 192, 192], replicated, may hold values from -0.078125 to 0.078125
- bias_one: float32 [192], replicated, may hold values from -3 to 3
- gain_two: float32 [192], replicated, may hold values from 0.5 to 1.5
- shift_two: float32 [192], replicated, may hold values from -3 to 3
- kernel_two: bfloat16 [3, 3, 3, 192, 192], replicated, may hold values from -0.078125 to 0.078125
- bias_two: float32 [192], replicated, may hold values from -3 to 3
- up_kernel: bfloat16 [3, 3, 192, 96], replicated, may hold values from -0.15625 to 0.15625
- up_bias: float32 [96], replicated, may hold values from -3 to 3
Outputs:
- decoded: bfloat16 [1, 8, 128, 64, 192], P(None, 'tm', 'tile')
The draws below stay inside these ranges and needn't reach their ends.
All inputs are finite; a program needn't handle non-finite values.
Results may differ from the reference program's by a relative error of at most 0.009.
Values may be sent and summed in bfloat16 or wider, within the bound.
A program may use at most 128 MiB of HBM per device.

```python
import jax
import jax.numpy as jnp
from jax import lax

C = 192
C2 = 96
G = 32
CLIPS = 1
W = 64
FRAMES = 8
H = 64


def draw_features(key, part):
    noise_key, row_key, col_key = jax.random.split(key, 3)
    shape_all = (CLIPS, FRAMES, H, W, C)
    row_place = jnp.arange(H, dtype=jnp.float32) / max(H - 1, 1)
    row_scale = 10.0 ** (jax.random.uniform(row_key, (H,), jnp.float32) - 0.5) * 3.0 ** (row_place - 1.0)
    col_scale = 10.0 ** (jax.random.uniform(col_key, (W,), jnp.float32) - 0.5)
    noise_draw = jax.random.truncated_normal(noise_key, -6.0, 6.0, shape_all, jnp.float32)
    scaled = noise_draw * row_scale[None, None, :, None, None] * col_scale[None, None, None, :, None]
    return scaled.astype(jnp.bfloat16)


def noise(rng, shape, width, most, held_as=jnp.bfloat16):
    drawn = width * jax.random.normal(rng, shape, jnp.float32)
    return jnp.clip(drawn, min=-most, max=most).astype(held_as)


def setup_inputs(seed: int = 0) -> dict:
    streams_of = jax.random.split(jax.random.key(seed), 12)
    features = draw_features(jax.random.fold_in(streams_of[11], 71), 0)
    gain_one = jnp.clip(1.0 + 0.1 * jax.random.normal(streams_of[1], (C,), jnp.float32), 0.5, 1.5)
    shift_one = noise(streams_of[2], (C,), 0.5, 3.0, jnp.float32)
    kernel_one = noise(streams_of[3], (3, 3, 3, C, C), (27 * C) ** -0.5, 0.078125)
    bias_one = noise(streams_of[4], (C,), 0.5, 3.0, jnp.float32)
    gain_two = jnp.clip(1.0 + 0.1 * jax.random.normal(streams_of[5], (C,), jnp.float32), 0.5, 1.5)
    shift_two = noise(streams_of[6], (C,), 0.5, 3.0, jnp.float32)
    kernel_two = noise(streams_of[7], (3, 3, 3, C, C), (27 * C) ** -0.5, 0.078125)
    bias_two = noise(streams_of[8], (C,), 0.5, 3.0, jnp.float32)
    up_kernel = noise(streams_of[9], (3, 3, C, C2), (9 * C) ** -0.5, 0.15625)
    up_bias = noise(streams_of[10], (C2,), 0.5, 3.0, jnp.float32)
    return {"features": features, "gain_one": gain_one, "shift_one": shift_one, "kernel_one": kernel_one, "bias_one": bias_one, "gain_two": gain_two, "shift_two": shift_two, "kernel_two": kernel_two, "bias_two": bias_two, "up_kernel": up_kernel, "up_bias": up_bias}


epsilon = 1e-06

def group_act(values_in, gain_vec, shift_vec):
    clip_count, frame_count, row_count, col_count, chan_count = values_in.shape
    grouped = values_in.reshape(clip_count, frame_count, row_count, col_count, G, chan_count // G)
    centre_value = lax.optimization_barrier(jnp.mean(grouped, axis=(2, 3, 5), keepdims=True))
    centered = grouped - centre_value
    spread_value = lax.optimization_barrier(jnp.mean(centered * centered, axis=(2, 3, 5), keepdims=True))
    normed = (centered * lax.rsqrt(spread_value + epsilon)).reshape(values_in.shape)
    return jax.nn.silu(normed * gain_vec + shift_vec).astype(jnp.bfloat16)

def causal_taps(padded, kernel, bias_term):
    clip_count, frame_span, row_span, col_count, chan_count = padded.shape
    out_frames = frame_span - 2
    out_rows = row_span - 2
    widened = jnp.pad(padded, ((0, 0), (0, 0), (0, 0), (1, 1), (0, 0)))
    accumulated = jnp.zeros((clip_count * out_frames * out_rows * col_count, kernel.shape[-1]), jnp.float32)
    for time_tap in range(3):
        for row_tap in range(3):
            slab_part = widened[:, time_tap:time_tap + out_frames, row_tap:row_tap + out_rows]
            stacked = jnp.concatenate([slab_part[:, :, :, col_tap:col_tap + col_count] for col_tap in range(3)], axis=-1)
            accumulated = accumulated + jnp.dot(stacked.reshape(-1, 3 * chan_count), kernel[time_tap, row_tap].reshape(3 * chan_count, -1), preferred_element_type=jnp.float32)
    return accumulated.reshape(clip_count, out_frames, out_rows, col_count, -1) + bias_term

def plane_taps(padded, kernel):
    clip_count, frame_count, row_span, col_span, chan_count = padded.shape
    out_rows = row_span - 2
    out_cols = col_span - 2
    accumulated = jnp.zeros((clip_count * frame_count * out_rows * out_cols, kernel.shape[-1]), jnp.float32)
    for row_tap in range(3):
        slab_part = padded[:, :, row_tap:row_tap + out_rows]
        stacked = jnp.concatenate([slab_part[:, :, :, col_tap:col_tap + out_cols] for col_tap in range(3)], axis=-1)
        accumulated = accumulated + jnp.dot(stacked.reshape(-1, 3 * chan_count), kernel[row_tap].reshape(3 * chan_count, -1), preferred_element_type=jnp.float32)
    return accumulated.reshape(clip_count, frame_count, out_rows, out_cols, -1)

def reference(features, gain_one, shift_one, kernel_one, bias_one, gain_two, shift_two, kernel_two, bias_two, up_kernel, up_bias):
    outputs = []
    for clip_index in range(CLIPS):
        source = features[clip_index:clip_index + 1].astype(jnp.float32)
        first_act = group_act(source, gain_one, shift_one)
        first_pad = jnp.pad(first_act, ((0, 0), (2, 0), (1, 1), (0, 0), (0, 0)))
        hidden = causal_taps(first_pad, kernel_one, bias_one).astype(jnp.bfloat16)
        second = group_act(hidden.astype(jnp.float32), gain_two, shift_two)
        second_pad = jnp.pad(second, ((0, 0), (2, 0), (1, 1), (0, 0), (0, 0)))
        joined = (source + causal_taps(second_pad, kernel_two, bias_two)).astype(jnp.bfloat16)
        doubled = jnp.repeat(jnp.repeat(joined, 2, axis=2), 2, axis=3)
        doubled_pad = jnp.pad(doubled, ((0, 0), (0, 0), (1, 1), (1, 1), (0, 0)))
        produced = (plane_taps(doubled_pad, up_kernel) + up_bias).astype(jnp.bfloat16)
        outputs.append(produced.reshape(1, FRAMES, 2 * H, W, 2 * C2))
    return jnp.concatenate(outputs, axis=0)
```

```python
import functools

import jax
import jax.numpy as jnp
from jax import lax
from jax.experimental import pallas as pl
from jax.experimental.pallas import tpu as pltpu
from jax.sharding import PartitionSpec as P

MESH = pl.DeviceIdType.MESH
G = 32
EPS = 1e-06
KP = 640
FT = 1
HIGH = lax.Precision.HIGHEST


def kernel(
    n,
    feat, g1, s1, k1, b1, g2, s2, k2, b2, uk, ub,
    out,
    x_ext, h_ext, j_ext, act, w1, w2, wup, ukv, sums, norm, st_own, st_prev,
    loc_sem, bulk_send, bulk_recv, own_send, own_recv, prev_send, prev_recv,
):
    frames, rows, cols, chans = feat.shape
    tm = lax.axis_index("tm")
    tile = lax.axis_index("tile")
    up_ok = tile > 0
    down_ok = tile < n - 1
    first = tm == 0
    later = tm > 0
    above = lax.rem(tile + n - 1, n)
    below = lax.rem(tile + 1, n)
    per = chans // G
    count = float(n * rows * cols * per)

    load_x = pltpu.make_async_copy(
        feat, x_ext.at[pl.ds(2, frames), pl.ds(1, rows)], loc_sem.at[0]
    )
    load_u = pltpu.make_async_copy(uk, ukv, loc_sem.at[1])
    load_1 = pltpu.make_async_copy(k1, w1.at[:, pl.ds(0, 3 * chans)], loc_sem.at[2])
    load_2 = pltpu.make_async_copy(k2, w2.at[:, pl.ds(0, 3 * chans)], loc_sem.at[3])
    load_x.start()
    load_u.start()
    load_1.start()
    load_2.start()

    barrier = pltpu.get_barrier_semaphore()
    for d in range(n):
        to = lax.rem(tile + d, n)
        pl.semaphore_signal(barrier, inc=1, device_id=(1 - tm, to), device_id_type=MESH)
        if d:
            pl.semaphore_signal(barrier, inc=1, device_id=(tm, to), device_id_type=MESH)

    def bulk(phase, src, dst):
        last = frames - 2

        def mk(i, s, t, who):
            return pltpu.make_async_remote_copy(
                src_ref=s, dst_ref=t,
                send_sem=bulk_send.at[phase, i], recv_sem=bulk_recv.at[phase, i],
                device_id=who, device_id_type=MESH,
            )

        f_all = pl.ds(2, frames)
        f_old = pl.ds(0, 2)
        return [
            (mk(0, src(slice(0, frames), rows - 1), dst.at[f_all, 0], (tm, below)), down_ok, up_ok),
            (mk(1, src(slice(0, frames), 0), dst.at[f_all, rows + 1], (tm, above)), up_ok, down_ok),
            (mk(2, src(slice(last, frames), slice(0, rows)), dst.at[f_old, pl.ds(1, rows)], (1, tile)), first, later),
            (mk(3, src(slice(last, frames), rows - 1), dst.at[f_old, 0], (1, below)), first & down_ok, later & up_ok),
            (mk(4, src(slice(last, frames), 0), dst.at[f_old, rows + 1], (1, above)), first & up_ok, later & down_ok),
        ]

    def rows_of(ref, f0, r0):
        def get(fs, rs):
            fi = pl.ds(f0 + fs.start, fs.stop - fs.start)
            ri = r0 + rs if isinstance(rs, int) else pl.ds(r0 + rs.start, rs.stop - rs.start)
            return ref.at[fi, ri]
        return get

    def start_all(copies):
        for copy, sends, _ in copies:
            pl.when(sends)(copy.start)

    def wait_recv_all(copies):
        for copy, _, gets in copies:
            pl.when(gets)(copy.wait_recv)

    def wait_send_all(copies):
        for copy, sends, _ in copies:
            pl.when(sends)(copy.wait_send)

    def stat_copies(phase):
        own, prev = [], []
        src = st_own.at[phase, 0, pl.ds(0, 2)]
        for d in range(n):
            to = lax.rem(tile + d, n)
            if d:
                own.append(pltpu.make_async_remote_copy(
                    src_ref=src, dst_ref=st_own.at[phase, d, pl.ds(0, 2)],
                    send_sem=own_send.at[phase, d], recv_sem=own_recv.at[phase, d],
                    device_id=(tm, to), device_id_type=MESH))
            prev.append(pltpu.make_async_remote_copy(
                src_ref=src, dst_ref=st_prev.at[phase, d, pl.ds(0, 2)],
                send_sem=prev_send.at[phase, d], recv_sem=prev_recv.at[phase, d],
                device_id=(1, to), device_id_type=MESH))
        return own, prev

    lane = lax.broadcasted_iota(jnp.int32, (chans, 128), 1)
    chan = lax.broadcasted_iota(jnp.int32, (chans, 128), 0)
    lane_t = lax.broadcasted_iota(jnp.int32, (128, chans), 0)
    chan_t = lax.broadcasted_iota(jnp.int32, (128, chans), 1)

    def gather_map(f):
        low = (lane - f * G) * per
        return jnp.where((chan >= low) & (chan < low + per), 1.0, 0.0)

    def spread_map(f):
        low = (lane_t - f * G) * per
        return jnp.where((chan_t >= low) & (chan_t < low + per), 1.0, 0.0)

    def put_sums(f, flat):
        total = jnp.sum(flat, axis=0, keepdims=True)
        square = jnp.sum(flat * flat, axis=0, keepdims=True)
        sums[f, 0:1] = total
        sums[f, 1:2] = square

    def send_stats(phase, copies):
        msg = jnp.zeros((2, 128), jnp.float32)
        for f in range(frames):
            msg = msg + jnp.dot(
                sums[f, 0:2], gather_map(f), precision=HIGH, preferred_element_type=jnp.float32
            )
        st_own[phase, 0, 0:2] = msg
        own, prev = copies
        for copy in own:
            copy.start()

        @pl.when(first)
        def _():
            for copy in prev:
                copy.start()

    def norm_rows(slot, total, f, gain):
        both = jnp.dot(
            total, spread_map(f), precision=HIGH, preferred_element_type=jnp.float32
        ) * (1.0 / count)
        mean = both[0:1]
        var = both[1:2] - mean * mean
        norm[slot, 0:1] = mean
        norm[slot, 1:2] = lax.rsqrt(var + EPS) * gain

    def take_stats(phase, copies, gain):
        own, prev = copies
        for copy in own:
            copy.wait_recv()
        total = st_own[phase, 0, 0:2]
        for d in range(1, n):
            total = total + st_own[phase, d, 0:2]
        for f in range(frames):
            norm_rows(2 + f, total, f, gain)

        @pl.when(later)
        def _():
            for copy in prev:
                copy.wait_recv()
            before = st_prev[phase, 0, 0:2]
            for d in range(1, n):
                before = before + st_prev[phase, d, 0:2]
            for f in range(2):
                norm_rows(f, before, frames - 2 + f, gain)

    def end_stats(copies):
        own, prev = copies
        for copy in own:
            copy.wait_send()

        @pl.when(first)
        def _():
            for copy in prev:
                copy.wait_send()

    col = lax.broadcasted_iota(jnp.int32, (cols, chans), 0)

    def put_shifted(f, r, value):
        left = jnp.where(col == 0, 0.0, pltpu.roll(value, 1, 0))
        right = jnp.where(col == cols - 1, 0.0, pltpu.roll(value, cols - 1, 0))
        act[f, r, :, 0:chans] = left.astype(jnp.bfloat16)
        act[f, r, :, chans:2 * chans] = value.astype(jnp.bfloat16)
        act[f, r, :, 2 * chans:3 * chans] = right.astype(jnp.bfloat16)

    def row_ok(r):
        return ((r > 0) | up_ok) & ((r <= rows) | down_ok)

    def build_act(src, shift):
        def step(i, carry):
            f = i // (rows + 2)
            r = lax.rem(i, rows + 2)
            ok = row_ok(r) & ((f > 1) | later)

            @pl.when(ok)
            def _():
                value = src[f, r].astype(jnp.float32)
                scaled = (value - norm[f, 0:1]) * norm[f, 1:2] + shift
                half = 0.5 * scaled
                put_shifted(f, r, half + half * jnp.tanh(half))

            @pl.when(jnp.logical_not(ok))
            def _():
                act[f, r, :, 0:3 * chans] = jnp.zeros((cols, 3 * chans), jnp.bfloat16)

            return carry

        lax.fori_loop(0, (frames + 2) * (rows + 2), step, 0)

    def conv(f, w):
        parts = [
            act[pl.ds(f + i, FT), j:j + rows].reshape(FT * rows * cols, KP)
            for i in range(3)
            for j in range(3)
        ]
        return jnp.dot(
            jnp.concatenate(parts, axis=-1),
            w[...].reshape(9 * KP, chans),
            preferred_element_type=jnp.float32,
        )

    pad = KP - 3 * chans
    act[:, :, :, 3 * chans:KP] = jnp.zeros((frames + 2, rows + 2, cols, pad), jnp.bfloat16)
    w1[:, 3 * chans:KP] = jnp.zeros((9, pad, chans), jnp.bfloat16)
    w2[:, 3 * chans:KP] = jnp.zeros((9, pad, chans), jnp.bfloat16)
    wup[:, :, 3 * chans:KP] = jnp.zeros((2, 2, pad, chans), jnp.bfloat16)

    load_x.wait()
    for f in range(frames):
        put_sums(f, x_ext[2 + f, 1:1 + rows].reshape(rows * cols, chans).astype(jnp.float32))

    bulk_one = bulk(0, rows_of(feat, 0, 0), x_ext)
    stats_one = stat_copies(0)
    pl.semaphore_wait(barrier, 2 * n - 1)
    send_stats(0, stats_one)
    start_all(bulk_one)

    load_u.wait()
    half = chans // 2

    def tap(j, k):
        return ukv[j, k].astype(jnp.float32)

    for r in range(2):
        for dy in range(2):
            js = ((0,), (1, 2)) if r == 0 else ((0, 1), (2,))
            line = [functools.reduce(jnp.add, [tap(j, k) for j in js[dy]]) for k in range(3)]
            zero = jnp.zeros_like(line[0])
            pieces = [
                (line[0], zero),
                (line[1] + line[2], line[0] + line[1]),
                (zero, line[2]),
            ]
            for dx, (even, odd) in enumerate(pieces):
                wup[r, dy, dx * chans:(dx + 1) * chans, 0:half] = even.astype(jnp.bfloat16)
                wup[r, dy, dx * chans:(dx + 1) * chans, half:chans] = odd.astype(jnp.bfloat16)

    take_stats(0, stats_one, g1[...])
    wait_recv_all(bulk_one)
    build_act(x_ext, s1[...])
    load_1.wait()

    def conv_one(i, carry):
        f = i * FT
        hidden = (conv(f, w1) + b1[...]).astype(jnp.bfloat16)
        h_ext[pl.ds(2 + f, FT), 1:1 + rows] = hidden.reshape(FT, rows, cols, chans)
        wide = hidden.astype(jnp.float32).reshape(FT, rows * cols, chans)
        for k in range(FT):
            put_sums(f + k, wide[k])
        return carry

    lax.fori_loop(0, frames // FT, conv_one, 0)

    bulk_two = bulk(1, rows_of(h_ext, 2, 1), h_ext)
    stats_two = stat_copies(1)
    send_stats(1, stats_two)
    start_all(bulk_two)
    take_stats(1, stats_two, g2[...])
    wait_recv_all(bulk_two)
    build_act(h_ext, s2[...])
    load_2.wait()

    def conv_two(i, carry):
        f = i * FT
        base = x_ext[pl.ds(2 + f, FT), 1:1 + rows].reshape(FT * rows * cols, chans)
        joined = base.astype(jnp.float32) + (conv(f, w2) + b2[...])
        j_ext[pl.ds(f, FT), 1:1 + rows] = joined.astype(jnp.bfloat16).reshape(FT, rows, cols, chans)
        return carry

    lax.fori_loop(0, frames // FT, conv_two, 0)

    def rim(i, row, to_row, who):
        return pltpu.make_async_remote_copy(
            src_ref=j_ext.at[:, row], dst_ref=j_ext.at[:, to_row],
            send_sem=bulk_send.at[2, i], recv_sem=bulk_recv.at[2, i],
            device_id=(tm, who), device_id_type=MESH,
        )

    bulk_three = [
        (rim(0, rows, 0, below), down_ok, up_ok),
        (rim(1, 1, rows + 1, above), up_ok, down_ok),
    ]
    start_all(bulk_three)
    wait_recv_all(bulk_three)

    def shift_rows(i, carry):
        f = i // (rows + 2)
        r = lax.rem(i, rows + 2)
        ok = row_ok(r)

        @pl.when(ok)
        def _():
            put_shifted(f, r, j_ext[f, r].astype(jnp.float32))

        @pl.when(jnp.logical_not(ok))
        def _():
            act[f, r, :, 0:3 * chans] = jnp.zeros((cols, 3 * chans), jnp.bfloat16)

        return carry

    lax.fori_loop(0, frames * (rows + 2), shift_rows, 0)

    def conv_up(i, carry):
        f = i * FT
        for r in range(2):
            parts = [
                act[pl.ds(f, FT), r + dy:r + dy + rows].reshape(FT * rows * cols, KP)
                for dy in range(2)
            ]
            made = jnp.dot(
                jnp.concatenate(parts, axis=-1),
                wup[r].reshape(2 * KP, chans),
                preferred_element_type=jnp.float32,
            ) + ub[...]
            made = made.astype(jnp.bfloat16).reshape(FT, rows, cols, chans)
            for y in range(rows):
                out[pl.ds(f, FT), 2 * y + r] = made[:, y]
        return carry

    lax.fori_loop(0, frames // FT, conv_up, 0)

    wait_send_all(bulk_one)
    wait_send_all(bulk_two)
    wait_send_all(bulk_three)
    end_stats(stats_one)
    end_stats(stats_two)


def solution(mesh):
    n = mesh.shape["tile"]

    def body(features, g1, s1, k1, b1, g2, s2, k2, b2, uk, ub):
        _, frames, rows, cols, chans = features.shape
        bf16, f32 = jnp.bfloat16, jnp.float32
        vmem = pl.BlockSpec(memory_space=pltpu.VMEM)
        hbm = pl.BlockSpec(memory_space=pl.ANY)
        vec = lambda v: v.reshape(1, -1)
        made = pl.pallas_call(
            functools.partial(kernel, n),
            out_shape=jax.ShapeDtypeStruct((frames, 2 * rows, cols, chans), bf16),
            in_specs=[hbm, vmem, vmem, hbm, vmem, vmem, vmem, hbm, vmem, hbm, vmem],
            out_specs=vmem,
            scratch_shapes=[
                pltpu.VMEM((frames + 2, rows + 2, cols, chans), bf16),
                pltpu.VMEM((frames + 2, rows + 2, cols, chans), bf16),
                pltpu.VMEM((frames, rows + 2, cols, chans), bf16),
                pltpu.VMEM((frames + 2, rows + 2, cols, KP), bf16),
                pltpu.VMEM((9, KP, chans), bf16),
                pltpu.VMEM((9, KP, chans), bf16),
                pltpu.VMEM((2, 2, KP, chans), bf16),
                pltpu.VMEM(uk.shape, bf16),
                pltpu.VMEM((frames, 8, chans), f32),
                pltpu.VMEM((frames + 2, 8, chans), f32),
                pltpu.VMEM((2, n, 8, 128), f32),
                pltpu.VMEM((2, n, 8, 128), f32),
                pltpu.SemaphoreType.DMA((4,)),
                pltpu.SemaphoreType.DMA((3, 5)),
                pltpu.SemaphoreType.DMA((3, 5)),
                pltpu.SemaphoreType.DMA((2, n)),
                pltpu.SemaphoreType.DMA((2, n)),
                pltpu.SemaphoreType.DMA((2, n)),
                pltpu.SemaphoreType.DMA((2, n)),
            ],
            compiler_params=pltpu.CompilerParams(
                collective_id=0, has_side_effects=True, vmem_limit_bytes=48 * 1024 * 1024
            ),
        )(
            features[0], vec(g1), vec(s1), k1.reshape(9, 3 * chans, chans), vec(b1),
            vec(g2), vec(s2), k2.reshape(9, 3 * chans, chans), vec(b2), uk,
            vec(jnp.concatenate([ub, ub])),
        )
        return made[None]

    return jax.shard_map(
        body,
        mesh=mesh,
        in_specs=(P(None, "tm", "tile", None, None),) + (P(),) * 10,
        out_specs=P(None, "tm", "tile", None, None),
        check_vma=False,
    )
```

```python
import functools

import jax
import jax.numpy as jnp
from jax import lax
from jax.experimental import pallas as pl
from jax.experimental.pallas import tpu as pltpu
from jax.sharding import PartitionSpec as P

MESH = pl.DeviceIdType.MESH
G = 32
EPS = 1e-06
KP = 640
ORDER = (2, 3, 0, 1)


def split_dot(value, picks):
    m = value.shape[0]
    high = value.astype(jnp.bfloat16).astype(jnp.float32)
    rest = value - high
    mid = rest.astype(jnp.bfloat16).astype(jnp.float32)
    low = rest - mid
    terms = jnp.concatenate([high, mid, low], axis=0).astype(jnp.bfloat16)
    made = jnp.dot(terms, picks, preferred_element_type=jnp.float32)
    return made[0:m] + made[m:2 * m] + made[2 * m:3 * m]


def kernel(
    n,
    feat, g1_h, s1_h, k1, b1_h, g2_h, s2_h, k2, b2_h, uk, ub_h,
    out,
    x_ext, h_ext, j_ext, act, jact, w1, w2, wup, ukv, vecs, ubv, norm, gmap, smap, st_own, st_prev,
    loc_sem, bulk_send, bulk_recv, own_send, own_recv, prev_send, prev_recv,
):
    frames, rows, cols, chans = feat.shape
    bf16, f32 = jnp.bfloat16, jnp.float32
    tm = lax.axis_index("tm")
    tile = lax.axis_index("tile")
    up_ok = tile > 0
    down_ok = tile < n - 1
    first = tm == 0
    later = tm > 0
    above = lax.rem(tile + n - 1, n)
    below = lax.rem(tile + 1, n)
    per = chans // G
    half = chans // 2
    inverse = 1.0 / float(n * rows * cols * per)
    old = frames - 2

    def local(i, s, d):
        copy = pltpu.make_async_copy(s, d, loc_sem.at[i])
        copy.start()
        return copy

    load_x = local(0, feat, x_ext.at[pl.ds(2, frames), pl.ds(1, rows)])

    barrier = pltpu.get_barrier_semaphore()
    for d in range(n):
        to = lax.rem(tile + d, n)
        pl.semaphore_signal(barrier, inc=1, device_id=(1 - tm, to), device_id_type=MESH)
        if d:
            pl.semaphore_signal(barrier, inc=1, device_id=(tm, to), device_id_type=MESH)

    load_u = local(1, uk, ukv)
    load_v = [
        local(4 + i, ref, vecs.at[i])
        for i, ref in enumerate((g1_h, s1_h, b1_h, g2_h, s2_h, b2_h))
    ]
    load_b = local(10, ub_h, ubv)
    load_1 = local(2, k1, w1.at[:, pl.ds(0, 3 * chans)])
    load_2 = local(3, k2, w2.at[:, pl.ds(0, 3 * chans)])

    def remote(slot, i, s, d, who):
        return pltpu.make_async_remote_copy(
            src_ref=s, dst_ref=d,
            send_sem=bulk_send.at[slot, i], recv_sem=bulk_recv.at[slot, i],
            device_id=who, device_id_type=MESH,
        )

    pending = []

    def start_all(copies):
        for copy, sends, _ in copies:
            pl.when(sends)(copy.start)
        pending.extend(copies)

    def wait_all(copies):
        for copy, _, gets in copies:
            pl.when(gets)(copy.wait_recv)

    def same_rows(slot, src, row0, f0, count, dst, g0):
        f, g = pl.ds(f0, count), pl.ds(g0, count)
        return [
            (remote(slot, 0, src.at[f, row0 + rows - 1], dst.at[g, 0], (tm, below)), down_ok, up_ok),
            (remote(slot, 1, src.at[f, row0], dst.at[g, rows + 1], (tm, above)), up_ok, down_ok),
        ]

    def next_frames(slot, src, row0, f0, count, dst, g0):
        f, g = pl.ds(f0, count), pl.ds(g0, count)
        return [
            (remote(slot, 2, src.at[f, pl.ds(row0, rows)], dst.at[g, pl.ds(1, rows)], (1, tile)), first, later),
            (remote(slot, 3, src.at[f, row0 + rows - 1], dst.at[g, 0], (1, below)), first & down_ok, later & up_ok),
            (remote(slot, 4, src.at[f, row0], dst.at[g, rows + 1], (1, above)), first & up_ok, later & down_ok),
        ]

    sent = []

    def own_copy(slot, d):
        return pltpu.make_async_remote_copy(
            src_ref=st_own.at[slot, 0, pl.ds(0, 2)], dst_ref=st_own.at[slot, d, pl.ds(0, 2)],
            send_sem=own_send.at[slot], recv_sem=own_recv.at[slot],
            device_id=(tm, lax.rem(tile + d, n)), device_id_type=MESH)

    def prev_copy(slot, to_slot, d):
        return pltpu.make_async_remote_copy(
            src_ref=st_own.at[slot, 0, pl.ds(0, 2)], dst_ref=st_prev.at[to_slot, d, pl.ds(0, 2)],
            send_sem=prev_send.at[to_slot], recv_sem=prev_recv.at[to_slot],
            device_id=(1, lax.rem(tile + d, n)), device_id_type=MESH)

    def own_all(slot):
        view = st_own.at[slot, pl.ds(1, n - 1), pl.ds(0, 2)]
        return pltpu.make_async_remote_copy(
            src_ref=view, dst_ref=view, send_sem=own_send.at[slot], recv_sem=own_recv.at[slot],
            device_id=(tm, below), device_id_type=MESH)

    def prev_all(slot):
        view = st_prev.at[slot, pl.ds(0, n), pl.ds(0, 2)]
        return pltpu.make_async_remote_copy(
            src_ref=view, dst_ref=view, send_sem=prev_send.at[slot], recv_sem=prev_recv.at[slot],
            device_id=(1, below), device_id_type=MESH)

    def send_sums(slot, message, to_slot):
        st_own[slot, 0, 0:2] = message
        for d in range(1, n):
            own_copy(slot, d).start()
        if to_slot is not None:
            @pl.when(first)
            def _():
                for d in range(n):
                    prev_copy(slot, to_slot, d).start()
        sent.append((slot, to_slot))

    def sums_of(flat):
        return jnp.concatenate(
            [jnp.sum(flat, axis=0, keepdims=True), jnp.sum(flat * flat, axis=0, keepdims=True)], axis=0
        )

    def norm_from(slot, total, f, gain):
        both = split_dot(total, smap[f]) * inverse
        mean = both[0:1]
        var = both[1:2] - mean * mean
        norm[slot, 0:1] = mean
        norm[slot, 1:2] = lax.rsqrt(var + EPS) * gain

    def own_total(slot):
        return jnp.sum(st_own[slot], axis=0)[0:2]

    def prev_total(slot):
        return jnp.sum(st_prev[slot], axis=0)[0:2]

    col = lax.broadcasted_iota(jnp.int32, (cols, chans), 0)

    def put_shifted(dst, f, r, value):
        left = jnp.where(col == 0, 0.0, pltpu.roll(value, 1, 0))
        right = jnp.where(col == cols - 1, 0.0, pltpu.roll(value, cols - 1, 0))
        dst[f, r, :, 0:chans] = left.astype(bf16)
        dst[f, r, :, chans:2 * chans] = value.astype(bf16)
        dst[f, r, :, 2 * chans:3 * chans] = right.astype(bf16)

    def act_frame(src, f, shift):
        mean, scale = norm[f, 0:1], norm[f, 1:2]
        for r in range(rows + 2):
            part = 0.5 * ((src[f, r].astype(f32) - mean) * scale + shift)
            value = part + part * jnp.tanh(part)
            ok = up_ok if r == 0 else down_ok if r == rows + 1 else None
            if f < 2:
                ok = later if ok is None else ok & later
            if ok is not None:
                value = jnp.where(ok, value, 0.0)
            put_shifted(act, f, r, value)

    def conv(f, w):
        parts = [
            act[f + i, j:j + rows].reshape(rows * cols, KP) for i in range(3) for j in range(3)
        ]
        return jnp.dot(
            jnp.concatenate(parts, axis=-1), w[...].reshape(9 * KP, chans), preferred_element_type=f32
        )

    lane = lax.broadcasted_iota(jnp.int32, (chans, 128), 1)
    chan = lax.broadcasted_iota(jnp.int32, (chans, 128), 0)
    lane_t = lax.broadcasted_iota(jnp.int32, (128, chans), 0)
    chan_t = lax.broadcasted_iota(jnp.int32, (128, chans), 1)
    for f in range(frames):
        low = (lane - f * G) * per
        gmap[f] = jnp.where((chan >= low) & (chan < low + per), 1.0, 0.0).astype(bf16)
        low = (lane_t - f * G) * per
        smap[f] = jnp.where((chan_t >= low) & (chan_t < low + per), 1.0, 0.0).astype(bf16)

    load_x.wait()
    message = jnp.zeros((2, 128), f32)
    for f in range(frames):
        flat = x_ext[2 + f, 1:1 + rows].reshape(rows * cols, chans).astype(f32)
        message = message + split_dot(sums_of(flat), gmap[f])

    own_one = same_rows(0, feat, 0, 0, frames, x_ext, 2)
    prev_one = next_frames(0, feat, 0, old, 2, x_ext, 0)
    pl.semaphore_wait(barrier, 2 * n - 1)
    send_sums(0, message, 0)
    start_all(own_one + prev_one)

    pad = KP - 3 * chans
    act[:, :, :, 3 * chans:KP] = jnp.zeros((frames + 2, rows + 2, cols, pad), bf16)
    jact[:, :, :, 3 * chans:KP] = jnp.zeros((frames, rows + 2, cols, pad), bf16)
    w1[:, 3 * chans:KP] = jnp.zeros((9, pad, chans), bf16)
    w2[:, 3 * chans:KP] = jnp.zeros((9, pad, chans), bf16)
    wup[:, :, 3 * chans:KP] = jnp.zeros((2, 2, pad, chans), bf16)
    load_u.wait()
    for r in range(2):
        for dy in range(2):
            js = (((0,), (1, 2)) if r == 0 else ((0, 1), (2,)))[dy]
            line = [
                functools.reduce(jnp.add, [ukv[j, k].astype(f32) for j in js]) for k in range(3)
            ]
            zero = jnp.zeros_like(line[0])
            pieces = [(line[0], zero), (line[1] + line[2], line[0] + line[1]), (zero, line[2])]
            for dx, (even, odd) in enumerate(pieces):
                wup[r, dy, dx * chans:(dx + 1) * chans, 0:half] = even.astype(bf16)
                wup[r, dy, dx * chans:(dx + 1) * chans, half:chans] = odd.astype(bf16)
    for copy in load_v:
        copy.wait()
    load_b.wait()
    vecs[6, :, 0:half] = ubv[...]
    vecs[6, :, half:chans] = ubv[...]
    load_1.wait()

    own_all(0).wait_recv()
    wait_all(own_one)
    gain, shift = vecs[0], vecs[1]
    total = own_total(0)
    for f in range(frames):
        norm_from(2 + f, total, f, gain)

    halos = {}

    def hidden_frame(f):
        hidden = (conv(f, w1) + vecs[2]).astype(bf16)
        h_ext[2 + f, 1:1 + rows] = hidden.reshape(rows, cols, chans)
        return split_dot(sums_of(hidden.astype(f32)), gmap[0])

    def hidden_send(f, message):
        send_sums(1 + f, message, 1 + f - old if f >= old else None)
        halos[f] = same_rows(1 + f, h_ext, 1, 2 + f, 1, h_ext, 2 + f)
        ahead = []
        if f >= old:
            ahead = next_frames(1 + f, h_ext, 1, 2 + f, 1, h_ext, f - old)
            halos[f - frames] = ahead
        start_all(ahead + halos[f])

    for f in (2, 3, 4):
        act_frame(x_ext, f, shift)
    message = hidden_frame(2)
    act_frame(x_ext, 5, shift)
    hidden_send(2, message)

    @pl.when(later)
    def _():
        prev_all(0).wait_recv()

    wait_all(prev_one)
    total = prev_total(0)
    for f in range(2):
        norm_from(f, total, old + f, gain)
    message = hidden_frame(3)
    for f in range(2):
        act_frame(x_ext, f, shift)
    hidden_send(3, message)
    hidden_send(0, hidden_frame(0))
    hidden_send(1, hidden_frame(1))

    gain, shift = vecs[3], vecs[4]

    def second_frame(f):
        own_all(1 + f).wait_recv()
        wait_all(halos[f])
        norm_from(2 + f, own_total(1 + f), 0, gain)
        act_frame(h_ext, 2 + f, shift)

    def joined_frame(f):
        base = x_ext[2 + f, 1:1 + rows].reshape(rows * cols, chans).astype(f32)
        joined = (base + (conv(f, w2) + vecs[5])).astype(bf16)
        j_ext[f, 1:1 + rows] = joined.reshape(rows, cols, chans)
        copies = same_rows(1 + frames + f, j_ext, 1, f, 1, j_ext, f)
        start_all(copies)
        wide = joined.astype(f32).reshape(rows, cols, chans)
        for r in range(rows):
            put_shifted(jact, f, 1 + r, wide[r])
        return copies

    second_frame(2)
    second_frame(3)

    @pl.when(later)
    def _():
        prev_all(1).wait_recv()
        prev_all(2).wait_recv()

    for f in range(2):
        wait_all(halos[old + f - frames])
    for f in range(2):
        norm_from(f, prev_total(1 + f), 0, gain)
        act_frame(h_ext, f, shift)
    second_frame(0)
    load_2.wait()
    rims = [joined_frame(0)]
    second_frame(1)
    rims += [joined_frame(f) for f in range(1, frames)]

    bias = vecs[6]
    for f in range(frames):
        wait_all(rims[f])
        top = jnp.where(up_ok, j_ext[f, 0].astype(f32), 0.0)
        bottom = jnp.where(down_ok, j_ext[f, rows + 1].astype(f32), 0.0)
        put_shifted(jact, f, 0, top)
        put_shifted(jact, f, rows + 1, bottom)
        for r in range(2):
            parts = [jact[f, r + dy:r + dy + rows].reshape(rows * cols, KP) for dy in range(2)]
            made = jnp.dot(
                jnp.concatenate(parts, axis=-1), wup[r].reshape(2 * KP, chans), preferred_element_type=f32
            ) + bias
            made = made.astype(bf16).reshape(rows, cols, chans)
            for y in range(rows):
                out[f, 2 * y + r] = made[y]

    for copy, sends, _ in pending:
        pl.when(sends)(copy.wait_send)
    for slot, to_slot in sent:
        own_all(slot).wait_send()
    @pl.when(first)
    def _():
        for slot, to_slot in sent:
            if to_slot is not None:
                prev_all(to_slot).wait_send()


def solution(mesh):
    n = mesh.shape["tile"]

    def body(features, g1, s1, k1, b1, g2, s2, k2, b2, uk, ub):
        _, frames, rows, cols, chans = features.shape
        bf16, f32 = jnp.bfloat16, jnp.float32
        hbm = pl.BlockSpec(memory_space=pltpu.HBM)
        vec = lambda v: v.reshape(1, -1)
        dma = pltpu.SemaphoreType.DMA
        made = pl.pallas_call(
            functools.partial(kernel, n),
            out_shape=jax.ShapeDtypeStruct((frames, 2 * rows, cols, chans), bf16),
            in_specs=[hbm] * 11,
            out_specs=pl.BlockSpec(memory_space=pltpu.VMEM),
            scratch_shapes=[
                pltpu.VMEM((frames + 2, rows + 2, cols, chans), bf16),
                pltpu.VMEM((frames + 2, rows + 2, cols, chans), bf16),
                pltpu.VMEM((frames, rows + 2, cols, chans), bf16),
                pltpu.VMEM((frames + 2, rows + 2, cols, KP), bf16),
                pltpu.VMEM((frames, rows + 2, cols, KP), bf16),
                pltpu.VMEM((9, KP, chans), bf16),
                pltpu.VMEM((9, KP, chans), bf16),
                pltpu.VMEM((2, 2, KP, chans), bf16),
                pltpu.VMEM(uk.shape, bf16),
                pltpu.VMEM((7, 1, chans), f32),
                pltpu.VMEM((1, chans // 2), f32),
                pltpu.VMEM((frames + 2, 8, chans), f32),
                pltpu.VMEM((frames, chans, 128), bf16),
                pltpu.VMEM((frames, 128, chans), bf16),
                pltpu.VMEM((1 + frames, n, 8, 128), f32),
                pltpu.VMEM((3, n, 8, 128), f32),
                dma((11,)),
                dma((1 + 2 * frames, 5)),
                dma((1 + 2 * frames, 5)),
                dma((1 + frames,)),
                dma((1 + frames,)),
                dma((3,)),
                dma((3,)),
            ],
            compiler_params=pltpu.CompilerParams(
                collective_id=0, has_side_effects=True, vmem_limit_bytes=56 * 1024 * 1024
            ),
        )(
            features[0], vec(g1), vec(s1), k1.reshape(9, 3 * chans, chans), vec(b1),
            vec(g2), vec(s2), k2.reshape(9, 3 * chans, chans), vec(b2), uk, vec(ub),
        )
        return made[None]

    return jax.shard_map(
        body,
        mesh=mesh,
        in_specs=(P(None, "tm", "tile", None, None),) + (P(),) * 10,
        out_specs=P(None, "tm", "tile", None, None),
        check_vma=False,
    )
```

```python
import functools

import jax
import jax.numpy as jnp
from jax import lax
from jax.experimental import pallas as pl
from jax.experimental.pallas import tpu as pltpu
from jax.sharding import PartitionSpec as P

MESH = pl.DeviceIdType.MESH
G = 32
EPS = 1e-06
KP = 640
ORDER = (2, 3, 0, 1)


def split_dot(value, picks):
    m = value.shape[0]
    high = value.astype(jnp.bfloat16).astype(jnp.float32)
    rest = value - high
    mid = rest.astype(jnp.bfloat16).astype(jnp.float32)
    low = rest - mid
    terms = jnp.concatenate([high, mid, low], axis=0).astype(jnp.bfloat16)
    made = jnp.dot(terms, picks, preferred_element_type=jnp.float32)
    return made[0:m] + made[m:2 * m] + made[2 * m:3 * m]


def kernel(
    n,
    feat, g1_h, s1_h, k1, b1_h, g2_h, s2_h, k2, b2_h, uk, ub_h,
    out,
    x_ext, h_ext, j_ext, act, jact, w1, w2, wup, ukv, vecs, ubv, norm, gmap, smap, st_own, st_prev, st_fwd, beside,
    loc_sem, bulk_send, bulk_recv, own_send, own_recv, prev_send, prev_recv,
):
    frames, rows, cols, chans = feat.shape
    bf16, f32 = jnp.bfloat16, jnp.float32
    tm = lax.axis_index("tm")
    tile = lax.axis_index("tile")
    up_ok = tile > 0
    down_ok = tile < n - 1
    first = tm == 0
    later = tm > 0
    above = lax.rem(tile + n - 1, n)
    below = lax.rem(tile + 1, n)
    per = chans // G
    half = chans // 2
    inverse = 1.0 / float(n * rows * cols * per)
    old = frames - 2

    def local(i, s, d):
        copy = pltpu.make_async_copy(s, d, loc_sem.at[i])
        copy.start()
        return copy

    load_x = local(0, feat, x_ext.at[pl.ds(2, frames), pl.ds(1, rows)])

    barrier = pltpu.get_barrier_semaphore()
    for d in range(1, n):
        to = lax.rem(tile + d, n)
        pl.semaphore_signal(barrier, inc=1, device_id=(tm, to), device_id_type=MESH)
    for to in (tile, above, below):
        pl.semaphore_signal(barrier, inc=1, device_id=(1 - tm, to), device_id_type=MESH)

    load_u = local(1, uk, ukv)
    load_v = [
        local(4 + i, ref, vecs.at[i])
        for i, ref in enumerate((g1_h, s1_h, b1_h, g2_h, s2_h, b2_h))
    ]
    load_b = local(10, ub_h, ubv)
    load_1 = local(2, k1, w1.at[:, pl.ds(0, 3 * chans)])
    load_2 = local(3, k2, w2.at[:, pl.ds(0, 3 * chans)])

    def remote(slot, i, s, d, who):
        return pltpu.make_async_remote_copy(
            src_ref=s, dst_ref=d,
            send_sem=bulk_send.at[slot, i], recv_sem=bulk_recv.at[slot, i],
            device_id=who, device_id_type=MESH,
        )

    pending = []

    def start_all(copies):
        for copy, sends, _ in copies:
            pl.when(sends)(copy.start)
        pending.extend(copies)

    def wait_all(copies):
        for copy, _, gets in copies:
            pl.when(gets)(copy.wait_recv)

    def same_rows(slot, src, row0, f0, count, dst, g0):
        f, g = pl.ds(f0, count), pl.ds(g0, count)
        return [
            (remote(slot, 0, src.at[f, row0 + rows - 1], dst.at[g, 0], (tm, below)), down_ok, up_ok),
            (remote(slot, 1, src.at[f, row0], dst.at[g, rows + 1], (tm, above)), up_ok, down_ok),
        ]

    def next_frames(slot, src, row0, f0, count, dst, g0):
        f, g = pl.ds(f0, count), pl.ds(g0, count)
        return [
            (remote(slot, 2, src.at[f, pl.ds(row0, rows)], dst.at[g, pl.ds(1, rows)], (1, tile)), first, later),
            (remote(slot, 3, src.at[f, row0 + rows - 1], dst.at[g, 0], (1, below)), first & down_ok, later & up_ok),
            (remote(slot, 4, src.at[f, row0], dst.at[g, rows + 1], (1, above)), first & up_ok, later & down_ok),
        ]

    sent = []

    def own_copy(slot, d):
        return pltpu.make_async_remote_copy(
            src_ref=st_own.at[slot, 0, pl.ds(0, 2)], dst_ref=st_own.at[slot, d, pl.ds(0, 2)],
            send_sem=own_send.at[slot], recv_sem=own_recv.at[slot],
            device_id=(tm, lax.rem(tile + d, n)), device_id_type=MESH)

    def forward(slot):
        return pltpu.make_async_remote_copy(
            src_ref=st_fwd.at[slot, pl.ds(0, 2)], dst_ref=st_prev.at[slot, pl.ds(0, 2)],
            send_sem=prev_send.at[slot], recv_sem=prev_recv.at[slot],
            device_id=(1, tile), device_id_type=MESH)

    def send_total(slot, total):
        st_fwd[slot, 0:2] = total
        pl.when(first)(forward(slot).start)

    def own_all(slot):
        view = st_own.at[slot, pl.ds(1, n - 1), pl.ds(0, 2)]
        return pltpu.make_async_remote_copy(
            src_ref=view, dst_ref=view, send_sem=own_send.at[slot], recv_sem=own_recv.at[slot],
            device_id=(tm, below), device_id_type=MESH)

    def send_sums(slot, message):
        st_own[slot, 0, 0:2] = message
        for d in range(1, n):
            own_copy(slot, d).start()
        sent.append(slot)

    def sums_of(flat):
        return jnp.concatenate(
            [jnp.sum(flat, axis=0, keepdims=True), jnp.sum(flat * flat, axis=0, keepdims=True)], axis=0
        )

    def norm_from(slot, total, f, gain):
        both = split_dot(total, smap[f]) * inverse
        mean = both[0:1]
        var = both[1:2] - mean * mean
        norm[slot, 0:1] = mean
        norm[slot, 1:2] = 0.5 * (lax.rsqrt(var + EPS) * gain)

    def own_total(slot):
        return jnp.sum(st_own[slot], axis=0)[0:2]

    def prev_total(slot):
        return st_prev[slot, 0:2]

    beside[:, 0:8] = jnp.zeros((rows + 2, 8, chans), f32)
    beside[:, 8 + cols:16 + cols] = jnp.zeros((rows + 2, 8, chans), f32)

    def put_shifted(dst, f, r, value):
        beside[r, 8:8 + cols] = value
        left = beside[r, 7:7 + cols]
        right = beside[r, 9:9 + cols]
        dst[f, r, :, 0:chans] = left.astype(bf16)
        dst[f, r, :, chans:2 * chans] = value.astype(bf16)
        dst[f, r, :, 2 * chans:3 * chans] = right.astype(bf16)

    def act_frame(src, f, shift):
        mean, scale = norm[f, 0:1], norm[f, 1:2]
        for r in range(rows + 2):
            part = (src[f, r].astype(f32) - mean) * scale + shift
            value = part + part * jnp.tanh(part)
            ok = up_ok if r == 0 else down_ok if r == rows + 1 else None
            if f < 2:
                ok = later if ok is None else ok & later
            if ok is not None:
                value = jnp.where(ok, value, 0.0)
            put_shifted(act, f, r, value)

    def conv(f, w):
        parts = [
            act[f + i, j:j + rows].reshape(rows * cols, KP) for i in range(3) for j in range(3)
        ]
        return jnp.dot(
            jnp.concatenate(parts, axis=-1), w[...].reshape(9 * KP, chans), preferred_element_type=f32
        )

    lane = lax.broadcasted_iota(jnp.int32, (chans, 128), 1)
    chan = lax.broadcasted_iota(jnp.int32, (chans, 128), 0)
    lane_t = lax.broadcasted_iota(jnp.int32, (128, chans), 0)
    chan_t = lax.broadcasted_iota(jnp.int32, (128, chans), 1)
    for f in range(frames):
        low = (lane - f * G) * per
        gmap[f] = jnp.where((chan >= low) & (chan < low + per), 1.0, 0.0).astype(bf16)
        low = (lane_t - f * G) * per
        smap[f] = jnp.where((chan_t >= low) & (chan_t < low + per), 1.0, 0.0).astype(bf16)

    load_x.wait()
    message = jnp.zeros((2, 128), f32)
    for f in range(frames):
        flat = x_ext[2 + f, 1:1 + rows].reshape(rows * cols, chans).astype(f32)
        message = message + split_dot(sums_of(flat), gmap[f])

    own_one = same_rows(0, feat, 0, 0, frames, x_ext, 2)
    prev_one = next_frames(0, feat, 0, old, 2, x_ext, 0)
    pl.semaphore_wait(barrier, n + 2)
    send_sums(0, message)
    start_all(own_one + prev_one)

    pad = KP - 3 * chans
    act[:, :, :, 3 * chans:KP] = jnp.zeros((frames + 2, rows + 2, cols, pad), bf16)
    jact[:, :, :, 3 * chans:KP] = jnp.zeros((frames, rows + 2, cols, pad), bf16)
    w1[:, 3 * chans:KP] = jnp.zeros((9, pad, chans), bf16)
    w2[:, 3 * chans:KP] = jnp.zeros((9, pad, chans), bf16)
    wup[:, :, 3 * chans:KP] = jnp.zeros((2, 2, pad, chans), bf16)
    load_u.wait()
    for r in range(2):
        for dy in range(2):
            js = (((0,), (1, 2)) if r == 0 else ((0, 1), (2,)))[dy]
            line = [
                functools.reduce(jnp.add, [ukv[j, k].astype(f32) for j in js]) for k in range(3)
            ]
            zero = jnp.zeros_like(line[0])
            pieces = [(line[0], zero), (line[1] + line[2], line[0] + line[1]), (zero, line[2])]
            for dx, (even, odd) in enumerate(pieces):
                wup[r, dy, dx * chans:(dx + 1) * chans, 0:half] = even.astype(bf16)
                wup[r, dy, dx * chans:(dx + 1) * chans, half:chans] = odd.astype(bf16)
    for copy in load_v:
        copy.wait()
    load_b.wait()
    vecs[6, :, 0:half] = ubv[...]
    vecs[6, :, half:chans] = ubv[...]
    load_1.wait()

    own_all(0).wait_recv()
    wait_all(own_one)
    gain, shift = vecs[0], 0.5 * vecs[1]
    total = own_total(0)
    send_total(0, total)
    for f in range(frames):
        norm_from(2 + f, total, f, gain)

    halos = {}

    def hidden_frame(f):
        hidden = (conv(f, w1) + vecs[2]).astype(bf16)
        h_ext[2 + f, 1:1 + rows] = hidden.reshape(rows, cols, chans)
        return split_dot(sums_of(hidden.astype(f32)), gmap[0])

    def hidden_send(f, message):
        send_sums(1 + f, message)
        halos[f] = same_rows(1 + f, h_ext, 1, 2 + f, 1, h_ext, 2 + f)
        ahead = []
        if f >= old:
            ahead = next_frames(1 + f, h_ext, 1, 2 + f, 1, h_ext, f - old)
            halos[f - frames] = ahead
        start_all(ahead + halos[f])

    for f in (2, 3, 4):
        act_frame(x_ext, f, shift)
    message = hidden_frame(2)
    act_frame(x_ext, 5, shift)
    hidden_send(2, message)

    @pl.when(later)
    def _():
        forward(0).wait_recv()

    wait_all(prev_one)
    total = prev_total(0)
    for f in range(2):
        norm_from(f, total, old + f, gain)
    message = hidden_frame(3)
    for f in range(2):
        act_frame(x_ext, f, shift)
    hidden_send(3, message)
    hidden_send(0, hidden_frame(0))
    hidden_send(1, hidden_frame(1))

    gain, shift = vecs[3], 0.5 * vecs[4]

    def second_frame(f):
        if f < old:
            own_all(1 + f).wait_recv()
            totals[f] = own_total(1 + f)
        wait_all(halos[f])
        norm_from(2 + f, totals[f], 0, gain)
        act_frame(h_ext, 2 + f, shift)

    def joined_frame(f):
        base = x_ext[2 + f, 1:1 + rows].reshape(rows * cols, chans).astype(f32)
        joined = (base + (conv(f, w2) + vecs[5])).astype(bf16)
        j_ext[f, 1:1 + rows] = joined.reshape(rows, cols, chans)
        copies = same_rows(1 + frames + f, j_ext, 1, f, 1, j_ext, f)
        start_all(copies)
        wide = joined.astype(f32).reshape(rows, cols, chans)
        for r in range(rows):
            put_shifted(jact, f, 1 + r, wide[r])
        return copies

    totals = {}
    for f in range(old, frames):
        own_all(1 + f).wait_recv()
        totals[f] = own_total(1 + f)
        send_total(1 + f - old, totals[f])
    second_frame(2)
    second_frame(3)

    @pl.when(later)
    def _():
        forward(1).wait_recv()
        forward(2).wait_recv()

    for f in range(2):
        wait_all(halos[old + f - frames])
    for f in range(2):
        norm_from(f, prev_total(1 + f), 0, gain)
        act_frame(h_ext, f, shift)
    second_frame(0)
    load_2.wait()
    rims = [joined_frame(0)]
    second_frame(1)
    rims += [joined_frame(f) for f in range(1, frames)]

    bias = vecs[6]
    for f in range(frames):
        wait_all(rims[f])
        top = jnp.where(up_ok, j_ext[f, 0].astype(f32), 0.0)
        bottom = jnp.where(down_ok, j_ext[f, rows + 1].astype(f32), 0.0)
        put_shifted(jact, f, 0, top)
        put_shifted(jact, f, rows + 1, bottom)
        for r in range(2):
            parts = [jact[f, r + dy:r + dy + rows].reshape(rows * cols, KP) for dy in range(2)]
            made = jnp.dot(
                jnp.concatenate(parts, axis=-1), wup[r].reshape(2 * KP, chans), preferred_element_type=f32
            ) + bias
            made = made.astype(bf16).reshape(rows, cols, chans)
            for y in range(rows):
                out[f, 2 * y + r] = made[y]

    for copy, sends, _ in pending:
        pl.when(sends)(copy.wait_send)
    for slot in sent:
        own_all(slot).wait_send()

    @pl.when(first)
    def _():
        for slot in range(3):
            forward(slot).wait_send()


def solution(mesh):
    n = mesh.shape["tile"]

    def body(features, g1, s1, k1, b1, g2, s2, k2, b2, uk, ub):
        _, frames, rows, cols, chans = features.shape
        bf16, f32 = jnp.bfloat16, jnp.float32
        hbm = pl.BlockSpec(memory_space=pltpu.HBM)
        vec = lambda v: v.reshape(1, -1)
        dma = pltpu.SemaphoreType.DMA
        made = pl.pallas_call(
            functools.partial(kernel, n),
            out_shape=jax.ShapeDtypeStruct((frames, 2 * rows, cols, chans), bf16),
            in_specs=[hbm] * 11,
            out_specs=pl.BlockSpec(memory_space=pltpu.VMEM),
            scratch_shapes=[
                pltpu.VMEM((frames + 2, rows + 2, cols, chans), bf16),
                pltpu.VMEM((frames + 2, rows + 2, cols, chans), bf16),
                pltpu.VMEM((frames, rows + 2, cols, chans), bf16),
                pltpu.VMEM((frames + 2, rows + 2, cols, KP), bf16),
                pltpu.VMEM((frames, rows + 2, cols, KP), bf16),
                pltpu.VMEM((9, KP, chans), bf16),
                pltpu.VMEM((9, KP, chans), bf16),
                pltpu.VMEM((2, 2, KP, chans), bf16),
                pltpu.VMEM(uk.shape, bf16),
                pltpu.VMEM((7, 1, chans), f32),
                pltpu.VMEM((1, chans // 2), f32),
                pltpu.VMEM((frames + 2, 8, chans), f32),
                pltpu.VMEM((frames, chans, 128), bf16),
                pltpu.VMEM((frames, 128, chans), bf16),
                pltpu.VMEM((1 + frames, n, 8, 128), f32),
                pltpu.VMEM((3, 8, 128), f32),
                pltpu.VMEM((3, 8, 128), f32),
                pltpu.VMEM((rows + 2, cols + 16, chans), f32),
                dma((11,)),
                dma((1 + 2 * frames, 5)),
                dma((1 + 2 * frames, 5)),
                dma((1 + frames,)),
                dma((1 + frames,)),
                dma((3,)),
                dma((3,)),
            ],
            compiler_params=pltpu.CompilerParams(
                collective_id=0, has_side_effects=True, vmem_limit_bytes=56 * 1024 * 1024
            ),
        )(
            features[0], vec(g1), vec(s1), k1.reshape(9, 3 * chans, chans), vec(b1),
            vec(g2), vec(s2), k2.reshape(9, 3 * chans, chans), vec(b2), uk, vec(ub),
        )
        return made[None]

    return jax.shard_map(
        body,
        mesh=mesh,
        in_specs=(P(None, "tm", "tile", None, None),) + (P(),) * 10,
        out_specs=P(None, "tm", "tile", None, None),
        check_vma=False,
    )
```

```python
import functools

import jax
import jax.numpy as jnp
from jax import lax
from jax.experimental import pallas as pl
from jax.experimental.pallas import tpu as pltpu
from jax.sharding import PartitionSpec as P

MESH = pl.DeviceIdType.MESH
G = 32
EPS = 1e-06
KP = 640
ORDER = (2, 3, 0, 1)


def split_dot(value, picks):
    m = value.shape[0]
    high = value.astype(jnp.bfloat16).astype(jnp.float32)
    rest = value - high
    mid = rest.astype(jnp.bfloat16).astype(jnp.float32)
    low = rest - mid
    terms = jnp.concatenate([high, mid, low], axis=0).astype(jnp.bfloat16)
    made = jnp.dot(terms, picks, preferred_element_type=jnp.float32)
    return made[0:m] + made[m:2 * m] + made[2 * m:3 * m]


def kernel(
    n,
    feat, g1_h, s1_h, k1, b1_h, g2_h, s2_h, k2, b2_h, uk, ub_h,
    out,
    x_ext, h_ext, j_ext, act, jact, w1, w2, wup, ukv, vecs, ubv, norm, gmap, smap, st_own, st_prev, st_fwd, beside,
    loc_sem, bulk_send, bulk_recv, own_send, own_recv, prev_send, prev_recv,
):
    frames, rows, cols, chans = feat.shape
    bf16, f32 = jnp.bfloat16, jnp.float32
    tm = lax.axis_index("tm")
    tile = lax.axis_index("tile")
    up_ok = tile > 0
    down_ok = tile < n - 1
    first = tm == 0
    later = tm > 0
    above = lax.rem(tile + n - 1, n)
    below = lax.rem(tile + 1, n)
    per = chans // G
    half = chans // 2
    inverse = 1.0 / float(n * rows * cols * per)
    old = frames - 2

    def local(i, s, d):
        copy = pltpu.make_async_copy(s, d, loc_sem.at[i])
        copy.start()
        return copy

    load_x = local(0, feat, x_ext.at[pl.ds(2, frames), pl.ds(1, rows)])

    barrier = pltpu.get_barrier_semaphore()
    for d in range(1, n):
        to = lax.rem(tile + d, n)
        pl.semaphore_signal(barrier, inc=1, device_id=(tm, to), device_id_type=MESH)
    for to in (tile, above, below):
        pl.semaphore_signal(barrier, inc=1, device_id=(1 - tm, to), device_id_type=MESH)

    load_u = local(1, uk, ukv)
    load_v = [
        local(4 + i, ref, vecs.at[i])
        for i, ref in enumerate((g1_h, s1_h, b1_h, g2_h, s2_h, b2_h))
    ]
    load_b = local(10, ub_h, ubv)
    load_1 = local(2, k1, w1.at[:, pl.ds(0, 3 * chans)])
    load_2 = local(3, k2, w2.at[:, pl.ds(0, 3 * chans)])

    def remote(slot, i, s, d, who):
        return pltpu.make_async_remote_copy(
            src_ref=s, dst_ref=d,
            send_sem=bulk_send.at[slot, i], recv_sem=bulk_recv.at[slot, i],
            device_id=who, device_id_type=MESH,
        )

    pending = []

    def start_all(copies):
        for copy, sends, _ in copies:
            pl.when(sends)(copy.start)
        pending.extend(copies)

    def wait_all(copies):
        for copy, _, gets in copies:
            pl.when(gets)(copy.wait_recv)

    def same_rows(slot, src, row0, f0, count, dst, g0):
        f, g = pl.ds(f0, count), pl.ds(g0, count)
        return [
            (remote(slot, 0, src.at[f, row0 + rows - 1], dst.at[g, 0], (tm, below)), down_ok, up_ok),
            (remote(slot, 1, src.at[f, row0], dst.at[g, rows + 1], (tm, above)), up_ok, down_ok),
        ]

    def next_frames(slot, src, row0, f0, count, dst, g0):
        f, g = pl.ds(f0, count), pl.ds(g0, count)
        return [
            (remote(slot, 2, src.at[f, pl.ds(row0, rows)], dst.at[g, pl.ds(1, rows)], (1, tile)), first, later),
            (remote(slot, 3, src.at[f, row0 + rows - 1], dst.at[g, 0], (1, below)), first & down_ok, later & up_ok),
            (remote(slot, 4, src.at[f, row0], dst.at[g, rows + 1], (1, above)), first & up_ok, later & down_ok),
        ]

    sent = []

    def own_copy(slot, d):
        return pltpu.make_async_remote_copy(
            src_ref=st_own.at[slot, 0, pl.ds(0, 2)], dst_ref=st_own.at[slot, d, pl.ds(0, 2)],
            send_sem=own_send.at[slot], recv_sem=own_recv.at[slot],
            device_id=(tm, lax.rem(tile + d, n)), device_id_type=MESH)

    def forward(slot):
        return pltpu.make_async_remote_copy(
            src_ref=st_fwd.at[slot, pl.ds(0, 2)], dst_ref=st_prev.at[slot, pl.ds(0, 2)],
            send_sem=prev_send.at[slot], recv_sem=prev_recv.at[slot],
            device_id=(1, tile), device_id_type=MESH)

    def send_total(slot, total):
        st_fwd[slot, 0:2] = total
        pl.when(first)(forward(slot).start)

    def own_all(slot):
        view = st_own.at[slot, pl.ds(1, n - 1), pl.ds(0, 2)]
        return pltpu.make_async_remote_copy(
            src_ref=view, dst_ref=view, send_sem=own_send.at[slot], recv_sem=own_recv.at[slot],
            device_id=(tm, below), device_id_type=MESH)

    def send_sums(slot, message):
        st_own[slot, 0, 0:2] = message
        for d in range(1, n):
            own_copy(slot, d).start()
        sent.append(slot)

    def sums_of(flat):
        return jnp.concatenate(
            [jnp.sum(flat, axis=0, keepdims=True), jnp.sum(flat * flat, axis=0, keepdims=True)], axis=0
        )

    def norm_from(slot, total, f, gain):
        both = split_dot(total, smap[f]) * inverse
        mean = both[0:1]
        var = both[1:2] - mean * mean
        norm[slot, 0:1] = mean
        norm[slot, 1:2] = 0.5 * (lax.rsqrt(var + EPS) * gain)

    def own_total(slot):
        return jnp.sum(st_own[slot], axis=0)[0:2]

    def prev_total(slot):
        return st_prev[slot, 0:2]

    beside[:, 0:8] = jnp.zeros((rows + 2, 8, chans), f32)
    beside[:, 8 + cols:16 + cols] = jnp.zeros((rows + 2, 8, chans), f32)

    def put_shifted(dst, f, r, value):
        beside[r, 8:8 + cols] = value
        left = beside[r, 7:7 + cols]
        right = beside[r, 9:9 + cols]
        dst[f, r, :, 0:chans] = left.astype(bf16)
        dst[f, r, :, chans:2 * chans] = value.astype(bf16)
        dst[f, r, :, 2 * chans:3 * chans] = right.astype(bf16)

    def act_frame(src, f, shift):
        mean, scale = norm[f, 0:1], norm[f, 1:2]
        for r in range(rows + 2):
            part = (src[f, r].astype(f32) - mean) * scale + shift
            value = part + part * jnp.tanh(part)
            ok = up_ok if r == 0 else down_ok if r == rows + 1 else None
            if f < 2:
                ok = later if ok is None else ok & later
            if ok is not None:
                value = jnp.where(ok, value, 0.0)
            put_shifted(act, f, r, value)

    def conv(f, w):
        parts = [
            act[f + i, j:j + rows].reshape(rows * cols, KP) for i in range(3) for j in range(3)
        ]
        return jnp.dot(
            jnp.concatenate(parts, axis=-1), w[...].reshape(9 * KP, chans), preferred_element_type=f32
        )

    lane = lax.broadcasted_iota(jnp.int32, (chans, 128), 1)
    chan = lax.broadcasted_iota(jnp.int32, (chans, 128), 0)
    lane_t = lax.broadcasted_iota(jnp.int32, (128, chans), 0)
    chan_t = lax.broadcasted_iota(jnp.int32, (128, chans), 1)
    for f in range(frames):
        low = (lane - f * G) * per
        gmap[f] = jnp.where((chan >= low) & (chan < low + per), 1.0, 0.0).astype(bf16)
        low = (lane_t - f * G) * per
        smap[f] = jnp.where((chan_t >= low) & (chan_t < low + per), 1.0, 0.0).astype(bf16)

    load_x.wait()
    message = jnp.zeros((2, 128), f32)
    for f in range(frames):
        flat = x_ext[2 + f, 1:1 + rows].reshape(rows * cols, chans).astype(f32)
        message = message + split_dot(sums_of(flat), gmap[f])

    own_one = same_rows(0, feat, 0, 0, frames, x_ext, 2)
    prev_one = next_frames(0, feat, 0, old, 2, x_ext, 0)
    pl.semaphore_wait(barrier, n + 2)
    send_sums(0, message)
    start_all(own_one + prev_one)

    pad = KP - 3 * chans
    act[:, :, :, 3 * chans:KP] = jnp.zeros((frames + 2, rows + 2, cols, pad), bf16)
    jact[:, :, :, 3 * chans:KP] = jnp.zeros((frames, rows + 2, cols, pad), bf16)
    w1[:, 3 * chans:KP] = jnp.zeros((9, pad, chans), bf16)
    w2[:, 3 * chans:KP] = jnp.zeros((9, pad, chans), bf16)
    wup[:, :, 3 * chans:KP] = jnp.zeros((2, 2, pad, chans), bf16)
    load_u.wait()
    for r in range(2):
        for dy in range(2):
            js = (((0,), (1, 2)) if r == 0 else ((0, 1), (2,)))[dy]
            line = [
                functools.reduce(jnp.add, [ukv[j, k].astype(f32) for j in js]) for k in range(3)
            ]
            zero = jnp.zeros_like(line[0])
            pieces = [(line[0], zero), (line[1] + line[2], line[0] + line[1]), (zero, line[2])]
            for dx, (even, odd) in enumerate(pieces):
                wup[r, dy, dx * chans:(dx + 1) * chans, 0:half] = even.astype(bf16)
                wup[r, dy, dx * chans:(dx + 1) * chans, half:chans] = odd.astype(bf16)
    for copy in load_v:
        copy.wait()
    load_b.wait()
    vecs[6, :, 0:half] = ubv[...]
    vecs[6, :, half:chans] = ubv[...]
    load_1.wait()

    own_all(0).wait_recv()
    wait_all(own_one)
    gain, shift = vecs[0], 0.5 * vecs[1]
    total = own_total(0)
    send_total(0, total)
    for f in range(frames):
        norm_from(2 + f, total, f, gain)

    halos = {}

    def hidden_frame(f):
        hidden = (conv(f, w1) + vecs[2]).astype(bf16)
        h_ext[2 + f, 1:1 + rows] = hidden.reshape(rows, cols, chans)
        return split_dot(sums_of(hidden.astype(f32)), gmap[0])

    def hidden_send(f, message):
        send_sums(1 + f, message)
        halos[f] = same_rows(1 + f, h_ext, 1, 2 + f, 1, h_ext, 2 + f)
        ahead = []
        if f >= old:
            ahead = next_frames(1 + f, h_ext, 1, 2 + f, 1, h_ext, f - old)
            halos[f - frames] = ahead
        start_all(ahead + halos[f])

    for f in (2, 3, 4):
        act_frame(x_ext, f, shift)
    message = hidden_frame(2)
    act_frame(x_ext, 5, shift)
    hidden_send(2, message)

    @pl.when(later)
    def _():
        forward(0).wait_recv()

    wait_all(prev_one)
    total = prev_total(0)
    for f in range(2):
        norm_from(f, total, old + f, gain)
    message = hidden_frame(3)
    for f in range(2):
        act_frame(x_ext, f, shift)
    hidden_send(3, message)
    hidden_send(0, hidden_frame(0))

    gain, shift = vecs[3], 0.5 * vecs[4]

    def second_frame(f):
        if f < old:
            own_all(1 + f).wait_recv()
            totals[f] = own_total(1 + f)
        wait_all(halos[f])
        norm_from(2 + f, totals[f], 0, gain)
        act_frame(h_ext, 2 + f, shift)

    def joined_frame(f):
        base = x_ext[2 + f, 1:1 + rows].reshape(rows * cols, chans).astype(f32)
        joined = (base + (conv(f, w2) + vecs[5])).astype(bf16)
        j_ext[f, 1:1 + rows] = joined.reshape(rows, cols, chans)
        copies = same_rows(1 + frames + f, j_ext, 1, f, 1, j_ext, f)
        start_all(copies)
        wide = joined.astype(f32).reshape(rows, cols, chans)
        for r in range(rows):
            put_shifted(jact, f, 1 + r, wide[r])
        return copies

    totals = {}

    def pass_on(f):
        own_all(1 + f).wait_recv()
        totals[f] = own_total(1 + f)
        send_total(1 + f - old, totals[f])

    pass_on(2)
    second_frame(2)
    hidden_send(1, hidden_frame(1))
    pass_on(3)

    @pl.when(later)
    def _():
        forward(1).wait_recv()
        forward(2).wait_recv()

    for f in range(2):
        wait_all(halos[old + f - frames])
    for f in range(2):
        norm_from(f, prev_total(1 + f), 0, gain)
        act_frame(h_ext, f, shift)
    second_frame(0)
    load_2.wait()
    second_frame(3)
    rims = [joined_frame(0)]
    second_frame(1)
    rims += [joined_frame(f) for f in range(1, frames)]

    bias = vecs[6]
    for f in range(frames):
        wait_all(rims[f])
        top = jnp.where(up_ok, j_ext[f, 0].astype(f32), 0.0)
        bottom = jnp.where(down_ok, j_ext[f, rows + 1].astype(f32), 0.0)
        put_shifted(jact, f, 0, top)
        put_shifted(jact, f, rows + 1, bottom)
        for r in range(2):
            parts = [jact[f, r + dy:r + dy + rows].reshape(rows * cols, KP) for dy in range(2)]
            made = jnp.dot(
                jnp.concatenate(parts, axis=-1), wup[r].reshape(2 * KP, chans), preferred_element_type=f32
            ) + bias
            made = made.astype(bf16).reshape(rows, cols, chans)
            for y in range(rows):
                out[f, 2 * y + r] = made[y]

    for copy, sends, _ in pending:
        pl.when(sends)(copy.wait_send)
    for slot in sent:
        own_all(slot).wait_send()

    @pl.when(first)
    def _():
        for slot in range(3):
            forward(slot).wait_send()


def solution(mesh):
    n = mesh.shape["tile"]

    def body(features, g1, s1, k1, b1, g2, s2, k2, b2, uk, ub):
        _, frames, rows, cols, chans = features.shape
        bf16, f32 = jnp.bfloat16, jnp.float32
        hbm = pl.BlockSpec(memory_space=pltpu.HBM)
        vec = lambda v: v.reshape(1, -1)
        dma = pltpu.SemaphoreType.DMA
        made = pl.pallas_call(
            functools.partial(kernel, n),
            out_shape=jax.ShapeDtypeStruct((frames, 2 * rows, cols, chans), bf16),
            in_specs=[hbm] * 11,
            out_specs=pl.BlockSpec(memory_space=pltpu.VMEM),
            scratch_shapes=[
                pltpu.VMEM((frames + 2, rows + 2, cols, chans), bf16),
                pltpu.VMEM((frames + 2, rows + 2, cols, chans), bf16),
                pltpu.VMEM((frames, rows + 2, cols, chans), bf16),
                pltpu.VMEM((frames + 2, rows + 2, cols, KP), bf16),
                pltpu.VMEM((frames, rows + 2, cols, KP), bf16),
                pltpu.VMEM((9, KP, chans), bf16),
                pltpu.VMEM((9, KP, chans), bf16),
                pltpu.VMEM((2, 2, KP, chans), bf16),
                pltpu.VMEM(uk.shape, bf16),
                pltpu.VMEM((7, 1, chans), f32),
                pltpu.VMEM((1, chans // 2), f32),
                pltpu.VMEM((frames + 2, 8, chans), f32),
                pltpu.VMEM((frames, chans, 128), bf16),
                pltpu.VMEM((frames, 128, chans), bf16),
                pltpu.VMEM((1 + frames, n, 8, 128), f32),
                pltpu.VMEM((3, 8, 128), f32),
                pltpu.VMEM((3, 8, 128), f32),
                pltpu.VMEM((rows + 2, cols + 16, chans), f32),
                dma((11,)),
                dma((1 + 2 * frames, 5)),
                dma((1 + 2 * frames, 5)),
                dma((1 + frames,)),
                dma((1 + frames,)),
                dma((3,)),
                dma((3,)),
            ],
            compiler_params=pltpu.CompilerParams(
                collective_id=0, has_side_effects=True, vmem_limit_bytes=56 * 1024 * 1024
            ),
        )(
            features[0], vec(g1), vec(s1), k1.reshape(9, 3 * chans, chans), vec(b1),
            vec(g2), vec(s2), k2.reshape(9, 3 * chans, chans), vec(b2), uk, vec(ub),
        )
        return made[None]

    return jax.shard_map(
        body,
        mesh=mesh,
        in_specs=(P(None, "tm", "tile", None, None),) + (P(),) * 10,
        out_specs=P(None, "tm", "tile", None, None),
        check_vma=False,
    )
```
